32 devices in a mesh: agg: 8 (over z, x), col: 4 (over y, core).
Axes of the slice: x: 2, y: 2, z: 4, core: 2. Of those that a mesh axis runs over, the one named last changes fastest.
Arguments:
- fine_tiles: bfloat16 [128, 4, 192, 192], P('agg', 'col')
- fine_cols: int32 [128, 4], P('agg', 'col'), may hold values from 0 to 127, as said below
- agg_of: int32 [128], P('agg'), may hold values from 0 to 31, as said below
- prolong: bfloat16 [128, 192, 192], P('agg'), may hold values from -0.21875 to 0.21875
- coarse_cols: int32 [32, 4], P('agg'), may hold values from 0 to 31, as said below
Outputs:
- coarse_tiles: float32 [32, 4, 192, 192], P('agg', 'col')
- factor_tiles: float32 [32, 4, 192, 192], P('agg', 'col')
The draws below stay inside these ranges and needn't reach their ends.
Inputs may be any that keep to these rules, and one draw needn't show every extreme that they name: Fine block row i belongs to an aggregate of its own index of agg: i // 16 * 4 <= agg_of[i] < i // 16 * 4 + 4; every aggregate has at least one fine row. `coarse_cols`: slot 0 of aggregate row c is c itself; the other slots are distinct aggregates c + o with 1 <= |o| <= 4. `fine_cols`: slot 0 of fine row i is i; for slots 1 and above the aggregate of the named fine row is one of the slots 1 and above of row agg_of[i] of coarse_cols.
All inputs are finite; a program needn't handle non-finite values.
Results may differ from the reference program's by a relative error of at most 0.0055.
Values may be sent and summed in bfloat16 or wider, within the bound.
A program may use at most 128 MiB of HBM per device.

```python
import math
import jax
import jax.numpy as jnp
from jax import lax

B = 192
NA = 4
NC = 4
COARSE_DEV = 4
FR_DEV = 16
SWEEPS = 2
FINE = 128
COARSE = 32
N_AGG = 8


def pattern_table(key):
    reach = COARSE_DEV
    row_ids = jnp.arange(COARSE, dtype=jnp.int32)
    offsets = jnp.concatenate([jnp.arange(-reach, 0, dtype=jnp.int32), jnp.arange(1, reach + 1, dtype=jnp.int32)])
    places = row_ids[:, None] + offsets[None, :]
    inside = (places >= 0) & (places < COARSE)
    positions = jnp.arange(2 * reach, dtype=jnp.int32)
    scores = jax.random.randint(jax.random.fold_in(key, 11), (COARSE, 2 * reach), 0, 1 << 20) * (2 * reach) + positions[None, :]
    scores = jnp.where(inside, scores, -1 - positions[None, :])
    unused, picked = lax.top_k(scores, NC - 1)
    chosen = jnp.take_along_axis(places, picked, axis=1)
    return jnp.concatenate([row_ids[:, None], chosen], axis=1).astype(jnp.int32)


def grouping(key):
    groups = COARSE // COARSE_DEV
    positions = jnp.arange(FR_DEV, dtype=jnp.int32)
    scores = jax.random.randint(jax.random.fold_in(key, 23), (groups, FR_DEV), 0, 1 << 20) * FR_DEV + positions[None, :]
    permuted = jnp.argsort(scores, axis=1, stable=True).astype(jnp.int32)
    extra = jax.random.randint(jax.random.fold_in(key, 29), (groups, FR_DEV), 0, COARSE_DEV)
    labels = jnp.where(positions[None, :] < COARSE_DEV, positions[None, :], extra)
    ranking = jnp.argsort(permuted, axis=1, stable=True).astype(jnp.int32)
    local_label = jnp.take_along_axis(labels, ranking, axis=1)
    owners = jnp.arange(groups, dtype=jnp.int32)[:, None] * COARSE_DEV
    return ((local_label + owners).reshape(-1).astype(jnp.int32), permuted)


def draw_coarse_cols(key, part):
    return pattern_table(key)


def draw_agg_of(key, part):
    assigned, permuted = grouping(key)
    return assigned


def draw_fine_cols(key, part):
    pattern = pattern_table(key)
    assigned, permuted = grouping(key)
    row_ids = jnp.arange(FINE, dtype=jnp.int32)
    picked = jax.random.randint(jax.random.fold_in(key, 31), (FINE, NA - 1), 1, NC)
    target = pattern[assigned[:, None], picked]
    host_dev = target // COARSE_DEV
    member = target % COARSE_DEV
    attempts = jax.random.randint(jax.random.fold_in(key, 37), (FINE, NA - 1, 8), 0, FR_DEV)
    guesses = host_dev[..., None] * FR_DEV + attempts
    matches = assigned[guesses] == target[..., None]
    first_hit = jnp.argmax(matches.astype(jnp.int32), axis=-1)
    found = jnp.take_along_axis(guesses, first_hit[..., None], axis=-1)[..., 0]
    fallback = host_dev * FR_DEV + permuted[host_dev, member]
    chosen = jnp.where(jnp.any(matches, axis=-1), found, fallback)
    return jnp.concatenate([row_ids[:, None], chosen], axis=1).astype(jnp.int32)


def draw_fine_tiles(key, part):
    spread = 4.0 / math.sqrt(B)
    tile_shape = (FINE, NA, B, B)
    noise = jax.random.normal(jax.random.fold_in(key, 41), tile_shape, jnp.float32) * spread
    lifting = jnp.exp(jax.random.uniform(jax.random.fold_in(key, 43), (FINE, B), jnp.float32, math.log(0.6), math.log(4.0)))
    identity = jnp.eye(B, dtype=jnp.float32)
    noise = noise.at[:, 0].add(lifting[:, :, None] * identity[None])
    return noise.astype(jnp.bfloat16)


def block_levels(stream_key, shape, pieces, low, largest):
    level, own = 1.0, jax.random.fold_in(stream_key, 6)
    for dim, parts in pieces:
        heights = jnp.exp(jax.random.uniform(jax.random.fold_in(own, dim), (parts,), jnp.float32, low / len(pieces), largest / len(pieces)))
        level = level * jnp.repeat(heights, shape[dim] // parts).reshape([-1 if axis == dim else 1 for axis in range(len(shape))])
    return level


def bell_draw(rng, dims, scale, limit, split=(), kind=jnp.bfloat16):
    drawn = jax.random.normal(rng, dims, jnp.float32) * scale
    if len(split) > 0:
        drawn = block_levels(rng, dims, split, -0.22, 0.18) * drawn
    return jnp.clip(drawn, min=-limit, max=limit).astype(kind)


def setup_inputs(seed: int = 0) -> dict:
    key_of = jax.random.split(jax.random.key(seed), 6)
    fine_tiles = draw_fine_tiles(jax.random.fold_in(key_of[5], 71), 0)
    fine_cols = draw_fine_cols(jax.random.fold_in(key_of[5], 71), 0)
    agg_of = draw_agg_of(jax.random.fold_in(key_of[5], 71), 0)
    prolong = bell_draw(key_of[3], (FINE, B, B), (B * FR_DEV // COARSE_DEV) ** -0.5, 0.21875, ((0, 8),))
    coarse_cols = draw_coarse_cols(jax.random.fold_in(key_of[5], 71), 0)
    return {"fine_tiles": fine_tiles, "fine_cols": fine_cols, "agg_of": agg_of, "prolong": prolong, "coarse_cols": coarse_cols}


HIGHEST = lax.Precision.HIGHEST


def relax_rows(target_coarse, target_old, target_cols, row_full, row_cols, ext_full, ext_cols, row_base, ext_base):
    row_count = row_cols.shape[0]
    ext_count = ext_full.shape[0]
    width = row_full.shape[-1]
    row_ids = row_base + jnp.arange(row_count, dtype=jnp.int32)
    lowest = jnp.minimum(row_ids[:, None], target_cols)
    prior_index = jnp.clip(row_cols - ext_base, 0, ext_count - 1).astype(jnp.int32)
    further = ext_full[prior_index]
    further_cols = ext_cols[prior_index]
    matched = (further_cols[:, None, :, :] == target_cols[:, :, None, None]) & (row_cols[:, None, :, None] < lowest[:, :, None, None])
    chosen = jnp.einsum('rqmn,rmnab->rqmab', matched.astype(jnp.float32), further, precision=HIGHEST)
    through = jnp.einsum('rmab,rqmbc->rqac', row_full, chosen, precision=HIGHEST)
    own_diag = row_full[:, 0]
    diag_index = jnp.clip(target_cols - ext_base, 0, ext_count - 1).astype(jnp.int32)
    their_diag = ext_full[diag_index, 0]
    upper_mask = jnp.arange(width)[None, :] > jnp.arange(width)[:, None]
    lower_mask = upper_mask.T
    upper_tile = row_ids[:, None] < target_cols
    lower_tile = row_ids[:, None] > target_cols
    on_diagonal = row_ids[:, None] == target_cols
    right_factor = jnp.where(upper_tile[:, :, None, None], target_old, jnp.where(upper_mask, own_diag, 0.0)[:, None])
    lower_term = jnp.einsum('rab,rqbc->rqac', jnp.where(lower_mask, own_diag, 0.0), right_factor, precision=HIGHEST)
    upper_term = jnp.einsum('rqab,rqbc->rqac', target_old, jnp.where(upper_mask, their_diag, 0.0), precision=HIGHEST)
    edge_term = jnp.where(lower_tile[:, :, None, None], upper_term, lower_term)
    residue = target_coarse - through - edge_term
    pivots = jnp.maximum(jnp.diagonal(their_diag, axis1=-2, axis2=-1), 1.0)
    scaled = lower_tile[:, :, None, None] | (on_diagonal[:, :, None, None] & lower_mask[None, None])
    return jnp.where(scaled, residue / pivots[:, :, None, :], residue)


def reference(fine_tiles, fine_cols, agg_of, prolong, coarse_cols):
    def coarse_block(block_index):
        start_row = (block_index * FR_DEV).astype(jnp.int32)
        tile_block = lax.dynamic_slice_in_dim(fine_tiles, start_row, FR_DEV, 0).astype(jnp.float32)
        columns = lax.dynamic_slice_in_dim(fine_cols, start_row, FR_DEV, 0)
        own_prolong = lax.dynamic_slice_in_dim(prolong, start_row, FR_DEV, 0).astype(jnp.float32)
        labels = lax.dynamic_slice_in_dim(agg_of, start_row, FR_DEV, 0)
        remote = prolong[columns].astype(jnp.float32)
        carried = jnp.einsum('isab,isbc->isac', tile_block, remote, precision=HIGHEST).astype(jnp.bfloat16)
        carried = lax.optimization_barrier(carried).astype(jnp.float32)
        lifted = jnp.einsum('iba,isbc->isac', own_prolong, carried, precision=HIGHEST)
        targets = agg_of[columns]
        owned_rows = (block_index * COARSE_DEV).astype(jnp.int32) + jnp.arange(COARSE_DEV, dtype=jnp.int32)
        row_pattern = lax.dynamic_slice_in_dim(coarse_cols, (block_index * COARSE_DEV).astype(jnp.int32), COARSE_DEV, 0)
        weights = ((labels[:, None] == owned_rows[None, :])[:, None, :, None] & (row_pattern[None, None, :, :] == targets[:, :, None, None])).astype(jnp.float32)
        return jnp.einsum('isrq,isac->rqac', weights, lifted, precision=HIGHEST)

    blocks = jnp.arange(N_AGG, dtype=jnp.int32)
    coarse = lax.map(coarse_block, blocks).reshape(COARSE, NC, B, B)
    factor = coarse
    for sweep_step in range(SWEEPS):
        def ilu_block(block_index, factor=factor):
            row_base = (block_index * COARSE_DEV).astype(jnp.int32)
            ext_base = jnp.maximum(row_base - COARSE_DEV, 0).astype(jnp.int32)
            ext_full = lax.dynamic_slice_in_dim(factor, ext_base, 2 * COARSE_DEV, 0)
            ext_cols = lax.dynamic_slice_in_dim(coarse_cols, ext_base, 2 * COARSE_DEV, 0)
            row_full = lax.dynamic_slice_in_dim(factor, row_base, COARSE_DEV, 0)
            row_cols = lax.dynamic_slice_in_dim(coarse_cols, row_base, COARSE_DEV, 0)
            row_coarse = lax.dynamic_slice_in_dim(coarse, row_base, COARSE_DEV, 0)
            return relax_rows(row_coarse, row_full, row_cols, row_full, row_cols, ext_full, ext_cols, row_base, ext_base)
        factor = lax.map(ilu_block, blocks).reshape(COARSE, NC, B, B)
    return coarse, factor
```

```python
import functools

import jax
import jax.numpy as jnp
from jax import lax
from jax.experimental import pallas as pl
from jax.experimental.pallas import tpu as pltpu
from jax.sharding import PartitionSpec as P

SWEEPS = 2
MESH = pl.DeviceIdType.MESH
BF = jnp.bfloat16
F32 = jnp.float32


def from_neighbours(values, axis):
    count = lax.axis_size(axis)
    up = lax.ppermute(values, axis, [(i, i + 1) for i in range(count - 1)])
    down = lax.ppermute(values, axis, [(i + 1, i) for i in range(count - 1)])
    return up, down


def make_tables(fine_cols, agg_of, coarse_cols, agg_index, col_index):
    rows = agg_of.shape[0]
    crows, slots = coarse_cols.shape
    i32 = jnp.int32
    packed = jnp.concatenate([agg_of, coarse_cols.reshape(-1)])
    before, after = from_neighbours(packed, "agg")
    labels = jnp.concatenate([before[:rows], agg_of, after[:rows]])
    ext_cols = jnp.concatenate([before[rows:].reshape(crows, slots), coarse_cols], axis=0)
    place = fine_cols[:, 0] - (agg_index - 1) * rows
    near_ids = jnp.arange(3 * rows, dtype=i32)
    target = jnp.sum(jnp.where(place[:, None] == near_ids[None, :], labels[None, :], 0), axis=1)
    row_base = agg_index * crows
    local = agg_of - row_base
    same = (local[:, None, None] == jnp.arange(crows, dtype=i32)[None, :, None]) & (
        coarse_cols[None] == target[:, None, None]
    )
    class_ids = jnp.arange(crows * slots, dtype=i32)
    member = same.reshape(rows, crows * slots)
    own_class = jnp.sum(jnp.where(member, class_ids[None, :], 0), axis=1)
    ids = jnp.arange(rows, dtype=i32)
    ahead = (own_class[None, :] < own_class[:, None]) | (
        (own_class[None, :] == own_class[:, None]) & (ids[None, :] < ids[:, None])
    )
    rank = jnp.sum(ahead.astype(i32), axis=1)
    at = rank[None, :] == ids[:, None]
    perm = jnp.sum(jnp.where(at, ids[None, :], 0), axis=1)
    place_sorted = jnp.sum(jnp.where(at, place[None, :], 0), axis=1)
    counts = jnp.sum(member.astype(i32), axis=0)
    upto = jnp.sum(
        (own_class[:, None] <= class_ids[None, :]).astype(i32), axis=0
    )
    last = jnp.maximum(upto - 1, 0)
    some = (counts > 0).astype(i32)
    starts = upto - counts
    first = jnp.sum(((starts[None, :] == ids[:, None]) & (counts > 0)[None, :]).astype(i32), axis=1)
    goes_on = 1 - first
    ext_count = 2 * crows
    ext_base = row_base - crows
    row_ids = row_base + jnp.arange(crows, dtype=i32)
    column = jnp.sum(
        jnp.where(jnp.arange(slots, dtype=i32)[None, :] == col_index, coarse_cols, 0), axis=1
    )
    lowest = jnp.minimum(row_ids, column)
    prior = jnp.clip(coarse_cols - ext_base, 0, ext_count - 1)
    pick = (prior[:, :, None] == jnp.arange(ext_count, dtype=i32)[None, None, :])
    further = jnp.sum(jnp.where(pick[..., None], ext_cols[None, None], 0), axis=2)
    hit = (further == column[:, None, None]) & (coarse_cols < lowest[:, None])[:, :, None]
    flag = jnp.any(hit, axis=2)
    slot_of = jnp.sum(jnp.where(hit, jnp.arange(slots, dtype=i32)[None, None, :], 0), axis=2)
    spot = ((prior // crows) * slots + slot_of) * crows + prior % crows
    spot = jnp.where(flag, spot, slots * crows)
    lower = row_ids > column
    upper = row_ids < column
    diag = jnp.clip(column - ext_base, 0, ext_count - 1)
    diag = jnp.where(lower, (diag // crows) * slots * crows + diag % crows, slots * crows + jnp.arange(crows, dtype=i32))
    return jnp.concatenate(
        [
            perm, place_sorted, goes_on,
            last, some,
            spot.reshape(-1), flag.astype(i32).reshape(-1),
            diag, lower.astype(i32), upper.astype(i32),
        ]
    ).astype(i32)


def kernel(
    dims, table, fine, own_prolong, coarse_out, factor_out,
    near, seg, rs_out, rs_in, ext_a, ext_b,
    copy_sem, h_send, h_recv, r_send, r_recv, a_send, a_recv, b_send, b_recv,
):
    groups, peers, rows, crows, slots, width = dims
    a = lax.axis_index("agg")
    c = lax.axis_index("col")
    c1 = c + 1 - 2 * (c % 2)
    c2 = (c + 2) % peers
    c3 = c2 + 1 - 2 * (c2 % 2)
    has_prev = a > 0
    has_next = a < groups - 1
    o_perm = 0
    o_place = o_perm + rows
    o_on = o_place + rows
    o_last = o_on + rows
    o_some = o_last + crows * slots
    o_spot = o_some + crows * slots
    o_flag = o_spot + crows * slots
    o_diag = o_flag + crows * slots
    o_lower = o_diag + crows
    o_upper = o_lower + crows

    barrier = pltpu.get_barrier_semaphore()
    for other in (c1, c2, c3):
        pl.semaphore_signal(barrier, inc=1, device_id=(a, other), device_id_type=MESH)

    @pl.when(has_prev)
    def _():
        pl.semaphore_signal(barrier, inc=1, device_id=(a - 1, c), device_id_type=MESH)

    @pl.when(has_next)
    def _():
        pl.semaphore_signal(barrier, inc=1, device_id=(a + 1, c), device_id_type=MESH)

    @pl.when(has_prev & has_next)
    def _():
        pl.semaphore_wait(barrier, 5)

    @pl.when(jnp.logical_not(has_prev & has_next))
    def _():
        pl.semaphore_wait(barrier, 4)

    def remote(src, dst, send, recv, device):
        return pltpu.make_async_remote_copy(
            src_ref=src, dst_ref=dst, send_sem=send, recv_sem=recv,
            device_id=device, device_id_type=MESH,
        )

    def spread(buf, at, size, chunks, send, recv, parts):
        def view(g, who, k):
            return buf.at[pl.ds(at(g, who) + k * size, size)]

        def hop(g, kind, who, k, device):
            return remote(
                view(g, who, k), view(g, who, k), send.at[g, kind, k], recv.at[g, kind, k], device
            )

        def each(body):
            for k in range(chunks):
                for g, condition, linked in parts:
                    if condition is None:
                        body(g, k, linked)
                    else:
                        pl.when(condition)(functools.partial(body, g, k, linked))

        def first(g, k, linked):
            if linked:
                hop(g, 0, c, k, (a, c1)).wait_recv()
            hop(g, 2, c, k, (a, c2)).start()
            hop(g, 1, c, k, (a, c1)).start()

        def second(g, k, linked):
            hop(g, 2, c2, k, (a, c2)).wait_recv()
            hop(g, 3, c2, k, (a, c1)).start()

        def third(g, k, linked):
            hop(g, 1, c1, k, (a, c1)).wait_recv()
            hop(g, 3, c3, k, (a, c1)).wait_recv()

        def done(g, k, linked):
            hop(g, 2, c, k, (a, c2)).wait_send()
            hop(g, 1, c, k, (a, c1)).wait_send()
            hop(g, 3, c2, k, (a, c1)).wait_send()

        each(first)
        each(second)
        each(third)
        return lambda: each(done)

    share = rows // peers
    h_chunks = h_send.shape[2]
    h_size = share // h_chunks

    def push(g, k, device):
        src = own_prolong.at[pl.ds(c * share + k * h_size, h_size)]
        dst = near.at[pl.ds((2 - g * 2) * rows + c * share + k * h_size, h_size)]
        return remote(src, dst, h_send.at[1 - g, 0, k], h_recv.at[1 - g, 0, k], device)

    def push_all(act):
        for k in range(h_chunks):
            @pl.when(has_next)
            def _():
                act(push(1, k, (a + 1, c)))

            @pl.when(has_prev)
            def _():
                act(push(0, k, (a - 1, c)))

    push_all(lambda copy: copy.start())
    keep = pltpu.make_async_copy(own_prolong, near.at[pl.ds(rows, rows)], copy_sem)
    keep.start()
    halo_done = spread(
        near, lambda g, who: g * 2 * rows + who * share, h_size, h_chunks, h_send, h_recv,
        ((0, has_prev, True), (1, has_next, True)),
    )
    keep.wait()

    def lift(k, total):
        i = table[o_perm + k]
        carried = jnp.dot(
            fine[i], near[table[o_place + k]], preferred_element_type=F32
        ).astype(BF)
        lifted = lax.dot_general(
            own_prolong[i], carried, (((0,), (0,)), ((), ())), preferred_element_type=F32
        )
        total = lifted + total * table[o_on + k].astype(F32)
        seg[k] = total
        return total

    lax.fori_loop(0, rows, lift, jnp.zeros((width, width), F32))

    def part(r, q):
        s = r * slots + q
        return seg[table[o_last + s]] * table[o_some + s].astype(F32)

    def give(q, sender):
        return remote(rs_out.at[q], rs_in.at[sender], r_send.at[q], r_recv.at[sender], (a, q))

    for q in range(1, slots):
        @pl.when((c > 0) & (c != q))
        def _():
            def fill(r, carry):
                rs_out[q, r] = part(r, q).astype(BF)
                return carry
            lax.fori_loop(0, crows, fill, 0)
            give(q, c).start()

    for s in range(1, slots):
        @pl.when((c > 0) & (c != s))
        def _():
            give(s, s).wait_recv()

    own_at = (slots + c) * crows

    @pl.when(c == 0)
    def _():
        def settle(r, carry):
            value = part(r, 0)
            coarse_out[r, 0] = value
            ext_a[own_at + r] = value.astype(BF)
            return carry
        lax.fori_loop(0, crows, settle, 0)

    for q in range(1, slots):
        @pl.when(c == q)
        def _():
            def settle(r, carry):
                value = part(r, q)
                for s in range(1, slots):
                    if s != q:
                        value = value + rs_in[s, r].astype(F32)
                coarse_out[r, 0] = value
                ext_a[own_at + r] = value.astype(BF)
                return carry
            lax.fori_loop(0, crows, settle, 0)

    chunks = a_send.shape[2]
    size = crows // chunks
    ids_r = lax.broadcasted_iota(jnp.int32, (width, width), 0)
    ids_c = lax.broadcasted_iota(jnp.int32, (width, width), 1)
    above = (ids_c > ids_r).astype(F32)
    below = (ids_c < ids_r).astype(F32)
    on = ids_c == ids_r

    finals = []
    for step in range(SWEEPS):
        ext, send, recv = ((ext_a, a_send, a_recv), (ext_b, b_send, b_recv))[step % 2]
        old = coarse_out if step == 0 else factor_out

        def onward(k, ext=ext, send=send, recv=recv):
            src = ext.at[pl.ds(own_at + k * size, size)]
            dst = ext.at[pl.ds(c * crows + k * size, size)]
            return remote(src, dst, send.at[0, 0, k], recv.at[0, 0, k], (a + 1, c))

        @pl.when(has_next)
        def _():
            for k in range(chunks):
                onward(k).start()

        finals.append(
            (
                onward,
                spread(
                    ext, lambda g, who: (g * slots + who) * crows, size, chunks, send, recv,
                    ((1, None, False), (0, has_prev, True)),
                ),
            )
        )

        def relax(r, carry):
            value = coarse_out[r, 0]
            for m in range(1, slots):
                s = r * slots + m
                left = ext[(slots + m) * crows + r]
                right = ext[table[o_spot + s]]
                value = value - table[o_flag + s].astype(F32) * jnp.dot(
                    left, right, preferred_element_type=F32
                )
            is_lower = table[o_lower + r].astype(F32)
            is_upper = table[o_upper + r].astype(F32)
            mine = old[r, 0]
            own_diag = ext[slots * crows + r].astype(F32)
            their_diag = ext[table[o_diag + r]].astype(F32)
            low = jnp.full((width, width), is_lower) > 0.5
            up = jnp.full((width, width), is_upper) > 0.5
            left = jnp.where(low, mine, own_diag * below)
            right = jnp.where(up, mine, their_diag * above)
            value = value - jnp.dot(
                left.astype(BF), right.astype(BF), preferred_element_type=F32
            )
            pivots = jnp.maximum(
                jnp.sum(jnp.where(on, their_diag, 0.0), axis=0, keepdims=True), 1.0
            )
            scaled = low | (jnp.logical_not(up) & (ids_c < ids_r))
            value = jnp.where(scaled, value / pivots, value)
            factor_out[r, 0] = value
            if step < SWEEPS - 1:
                following = (ext_a, ext_b)[(step + 1) % 2]
                following[own_at + r] = value.astype(BF)
            return carry

        lax.fori_loop(0, crows, relax, 0)

    push_all(lambda copy: copy.wait_send())
    halo_done()
    for q in range(1, slots):
        @pl.when((c > 0) & (c != q))
        def _():
            give(q, c).wait_send()
    for onward, finished in finals:
        @pl.when(has_next)
        def _():
            for k in range(chunks):
                onward(k).wait_send()
        finished()


def on_device(groups, peers, fine_tiles, fine_cols, agg_of, prolong, coarse_cols):
    rows, width = prolong.shape[0], prolong.shape[-1]
    crows, slots = coarse_cols.shape
    assert SWEEPS == 2 and slots == peers == 4 and fine_tiles.shape[1] == 1
    table = make_tables(
        fine_cols, agg_of, coarse_cols, lax.axis_index("agg"), lax.axis_index("col")
    )
    h_chunks, chunks = 2, 2
    dma = pltpu.SemaphoreType.DMA
    tile = (width, width)
    out = jax.ShapeDtypeStruct((crows, 1) + tile, F32)
    vmem = pl.BlockSpec(memory_space=pltpu.VMEM)
    return pl.pallas_call(
        functools.partial(kernel, (groups, peers, rows, crows, slots, width)),
        out_shape=(out, out),
        in_specs=[pl.BlockSpec(memory_space=pltpu.SMEM), vmem, vmem],
        out_specs=(vmem, vmem),
        scratch_shapes=[
            pltpu.VMEM((3 * rows,) + tile, BF),
            pltpu.VMEM((rows,) + tile, F32),
            pltpu.VMEM((slots, crows) + tile, BF),
            pltpu.VMEM((slots, crows) + tile, BF),
            pltpu.VMEM((2 * slots * crows,) + tile, BF),
            pltpu.VMEM((2 * slots * crows,) + tile, BF),
            dma(()),
            dma((2, 4, h_chunks)), dma((2, 4, h_chunks)),
            dma((slots,)), dma((slots,)),
            dma((2, 4, chunks)), dma((2, 4, chunks)),
            dma((2, 4, chunks)), dma((2, 4, chunks)),
        ],
        compiler_params=pltpu.CompilerParams(
            collective_id=0, has_side_effects=True, vmem_limit_bytes=48 * 1024 * 1024
        ),
    )(table, fine_tiles.reshape((rows,) + tile), prolong)


def solution(mesh):
    in_specs = (
        P("agg", "col", None, None),
        P("agg", "col"),
        P("agg"),
        P("agg", None, None),
        P("agg", None),
    )
    out_specs = (P("agg", "col", None, None), P("agg", "col", None, None))
    return jax.shard_map(
        functools.partial(on_device, mesh.shape["agg"], mesh.shape["col"]),
        mesh=mesh, in_specs=in_specs, out_specs=out_specs, check_vma=False,
    )
```

```python
import functools

import jax
import jax.numpy as jnp
from jax import lax
from jax.experimental import pallas as pl
from jax.experimental.pallas import tpu as pltpu
from jax.sharding import PartitionSpec as P

SWEEPS = 2
MESH = pl.DeviceIdType.MESH
BF = jnp.bfloat16
F32 = jnp.float32


def pack(tile, dtype):
    width = tile.shape[-1]
    lanes = 2 * width // 3
    half = width // 2
    rest = tile[:, lanes:]
    return tile[:, :lanes].astype(dtype), jnp.concatenate([rest[:half], rest[half:]], axis=1).astype(dtype)


def put(ref, index, tile):
    left, rest = pack(tile, ref.dtype)
    width = tile.shape[-1]
    ref[index, 0:width] = left
    ref[index, width:] = rest


def unpack(tile, width):
    half = width // 2
    rest = tile[width:]
    fold = width - tile.shape[-1]
    right = jnp.concatenate([rest[:, :fold], rest[:, fold:]], axis=0)
    return jnp.concatenate([tile[:width], right], axis=1)


def kernel(
    dims, ints, fine_hbm, prolong_hbm, coarse_out, factor_out,
    fine, own_prolong, near, seg, rs_out, rs_in, ext_a, ext_b, tab_v, tab, cls, order, table,
    in_sem, t_sem, t_send, t_recv,
    h_send, h_recv, r_send, r_recv, a_send, a_recv, b_send, b_recv,
):
    groups, peers, rows, crows, slots, width = dims
    a = lax.axis_index("agg")
    c = lax.axis_index("col")
    c1 = c + 1 - 2 * (c % 2)
    c2 = (c + 2) % peers
    c3 = c2 + 1 - 2 * (c2 % 2)
    has_prev = a > 0
    has_next = a < groups - 1
    share = rows // peers
    o_coarse = rows
    o_fine = o_coarse + crows * slots
    o_last = 0
    o_some = o_last + crows * slots
    o_spot = o_some + crows * slots
    o_flag = o_spot + crows * slots
    o_diag = o_flag + crows * slots

    take_share = pltpu.make_async_copy(
        prolong_hbm.at[pl.ds(c * share, share)],
        own_prolong.at[pl.ds(c * share, share)], in_sem.at[0],
    )
    take_share.start()

    def take_other(j):
        part_of = (c + j) % peers
        return pltpu.make_async_copy(
            prolong_hbm.at[pl.ds(part_of * share, share)],
            own_prolong.at[pl.ds(part_of * share, share)], in_sem.at[j],
        )

    for j in range(1, peers):
        take_other(j).start()
    take_fine = pltpu.make_async_copy(fine_hbm, fine, in_sem.at[peers])
    take_fine.start()

    barrier = pltpu.get_barrier_semaphore()
    for other in (c1, c2, c3):
        pl.semaphore_signal(barrier, inc=1, device_id=(a, other), device_id_type=MESH)

    @pl.when(has_prev)
    def _():
        pl.semaphore_signal(barrier, inc=1, device_id=(a - 1, c), device_id_type=MESH)

    @pl.when(has_next)
    def _():
        pl.semaphore_signal(barrier, inc=1, device_id=(a + 1, c), device_id_type=MESH)

    def remote(src, dst, send, recv, device):
        return pltpu.make_async_remote_copy(
            src_ref=src, dst_ref=dst, send_sem=send, recv_sem=recv,
            device_id=device, device_id_type=MESH,
        )

    def pack_own(first):
        def body(k, carry):
            put(near, rows + first + k, own_prolong[first + k].astype(F32))
            return carry
        lax.fori_loop(0, share, body, 0)

    take_share.wait()
    pack_own(c * share)

    @pl.when(has_prev & has_next)
    def _():
        pl.semaphore_wait(barrier, 5)

    @pl.when(jnp.logical_not(has_prev & has_next))
    def _():
        pl.semaphore_wait(barrier, 4)

    def ints_to(g, device):
        return remote(ints, tab_v.at[2 - 2 * g], t_send.at[g], t_recv.at[1 - g], device)

    def push(g, k, device):
        src = near.at[pl.ds(rows + c * share + k, 1)]
        dst = near.at[pl.ds((2 - g * 2) * rows + c * share + k, 1)]
        return remote(src, dst, h_send.at[1 - g, 0, k], h_recv.at[1 - g, 0, k], device)

    def push_all(act):
        @pl.when(has_next)
        def _():
            act(ints_to(1, (a + 1, c)))

        @pl.when(has_prev)
        def _():
            act(ints_to(0, (a - 1, c)))

        for k in range(share):
            @pl.when(has_next)
            def _():
                act(push(1, k, (a + 1, c)))

            @pl.when(has_prev)
            def _():
                act(push(0, k, (a - 1, c)))

    push_all(lambda copy: copy.start())
    for j in range(1, peers):
        take_other(j).wait()
        pack_own(((c + j) % peers) * share)

    def spreader(buf, at, send, recv):
        def hop(g, kind, who, k, device):
            view = buf.at[pl.ds(at(g, who) + k, 1)]
            return remote(view, view, send.at[g, kind, k], recv.at[g, kind, k], device)

        class Steps:
            def share(g, k):
                hop(g, 2, c, k, (a, c2)).start()
                hop(g, 1, c, k, (a, c1)).start()

            def first(g, k):
                hop(g, 0, c, k, (a, c1)).wait_recv()
                Steps.share(g, k)

            def second(g, k):
                hop(g, 2, c2, k, (a, c2)).wait_recv()
                hop(g, 3, c2, k, (a, c1)).start()

            def third(g, k):
                hop(g, 1, c1, k, (a, c1)).wait_recv()
                hop(g, 3, c3, k, (a, c1)).wait_recv()

            def done(g, k):
                hop(g, 2, c, k, (a, c2)).wait_send()
                hop(g, 1, c, k, (a, c1)).wait_send()
                hop(g, 3, c2, k, (a, c1)).wait_send()

        return Steps

    halo = spreader(near, lambda g, who: g * 2 * rows + who * share, h_send, h_recv)
    sides = ((0, has_prev), (1, has_next))

    def each_side(step):
        for k in range(share):
            for g, condition in sides:
                pl.when(condition)(functools.partial(step, g, k))

    def to_scalar(g):
        return pltpu.make_async_copy(tab_v.at[g], tab.at[g], t_sem.at[g])

    own_ints = pltpu.make_async_copy(ints, tab.at[1], t_sem.at[1])
    own_ints.start()

    each_side(halo.first)
    own_ints.wait()

    @pl.when(has_prev)
    def _():
        ints_to(1, (a - 1, c)).wait_recv()
        to_scalar(0).start()
        to_scalar(0).wait()

    @pl.when(has_next)
    def _():
        ints_to(0, (a + 1, c)).wait_recv()
        to_scalar(2).start()
        to_scalar(2).wait()

    row_base = a * crows
    ext_base = row_base - crows

    def mine(k):
        return tab[1, 0, k]

    def place_of(i):
        return mine(o_fine + i) - (a - 1) * rows

    def classify(i, carry):
        place = jnp.clip(place_of(i), 0, 3 * rows - 1)
        target = tab[place // rows, 0, place % rows]
        r = jnp.clip(mine(i) - row_base, 0, crows - 1)
        q = 0
        for s in range(1, slots):
            q = jnp.where(mine(o_coarse + r * slots + s) == target, s, q)
        cls[i] = (r * slots + q) * rows + i
        return carry

    lax.fori_loop(0, rows, classify, 0)

    def rank(i, carry):
        key = cls[i]
        below = 0
        for j in range(rows):
            below = below + jnp.where(cls[j] < key, 1, 0)
        order[rows + i] = below
        return carry

    lax.fori_loop(0, rows, rank, 0)

    def place_key(k, carry):
        key = 0
        for i in range(rows):
            key = key + jnp.where(order[rows + i] == k, cls[i], 0)
        order[k] = key
        return carry

    lax.fori_loop(0, rows, place_key, 0)

    def ends(s, carry):
        upto = 0
        some = 0
        for i in range(rows):
            own_class = cls[i] // rows
            upto = upto + jnp.where(own_class <= s, 1, 0)
            some = jnp.where(own_class == s, 1, some)
        table[o_last + s] = jnp.maximum(upto - 1, 0)
        table[o_some + s] = some
        return carry

    lax.fori_loop(0, crows * slots, ends, 0)

    def ties(r, carry):
        row = row_base + r
        column = mine(o_coarse + r * slots + c)
        lowest = jnp.minimum(row, column)
        for m in range(1, slots):
            prior = mine(o_coarse + r * slots + m)
            k = jnp.clip(prior - ext_base, 0, 2 * crows - 1)
            g = k // crows
            slot = 0
            found = 0
            for n in range(slots):
                same = tab[g, 0, o_coarse + (k % crows) * slots + n] == column
                slot = jnp.where(same, n, slot)
                found = jnp.where(same, 1, found)
            found = jnp.where(prior < lowest, found, 0)
            spot = (g * slots + slot) * crows + k % crows
            table[o_spot + r * slots + m] = jnp.where(found == 1, spot, slots * crows)
            table[o_flag + r * slots + m] = found
        k = jnp.clip(column - ext_base, 0, 2 * crows - 1)
        table[o_diag + r] = jnp.where(
            column < row, (k // crows) * slots * crows + k % crows, slots * crows + r
        )
        return carry

    lax.fori_loop(0, crows, ties, 0)

    each_side(halo.second)
    take_fine.wait()
    each_side(halo.third)

    def lift(k, total):
        key = order[k]
        i = key % rows
        earlier = order[jnp.maximum(k - 1, 0)]
        goes_on = jnp.where(earlier // rows == key // rows, 1, 0)
        place = jnp.clip(place_of(i), 0, 3 * rows - 1)
        carried = jnp.dot(
            fine[i], unpack(near[place], width), preferred_element_type=F32
        ).astype(BF)
        lifted = lax.dot_general(
            own_prolong[i], carried, (((0,), (0,)), ((), ())), preferred_element_type=F32
        )
        total = lifted + total * goes_on.astype(F32)
        seg[k] = total
        return total

    lax.fori_loop(0, rows, lift, jnp.zeros((width, width), F32))

    def part(r, q):
        s = r * slots + q
        return seg[table[o_last + s]] * table[o_some + s].astype(F32)

    others = slots - 1

    def partner(j):
        return 1 + (c - 1 + j) % others

    def give(j, r):
        return remote(
            rs_out.at[pl.ds(j * crows + r, 1)], rs_in.at[pl.ds((others - j) * crows + r, 1)],
            r_send.at[j, r], r_recv.at[others - j, r], (a, partner(j)),
        )

    @pl.when(c > 0)
    def _():
        for r in range(crows):
            for j in range(1, others):
                put(rs_out, j * crows + r, part(r, partner(j)))
                give(j, r).start()

    own_at = (slots + c) * crows
    exts = (ext_a, ext_b)
    gather = [
        spreader(ext, lambda g, who: (g * slots + who) * crows, send, recv)
        for ext, send, recv in ((ext_a, a_send, a_recv), (ext_b, b_send, b_recv))
    ]

    def onward(step, r):
        send, recv = ((a_send, a_recv), (b_send, b_recv))[step]
        ext = exts[step]
        return remote(
            ext.at[pl.ds(own_at + r, 1)], ext.at[pl.ds(c * crows + r, 1)],
            send.at[0, 0, r], recv.at[0, 0, r], (a + 1, c),
        )

    def send_row(step, r):
        gather[step].share(1, r)

        @pl.when(has_next)
        def _():
            onward(step, r).start()

    for r in range(crows):
        @pl.when(c == 0)
        def _():
            value = part(r, 0)
            coarse_out[r, 0] = value
            put(ext_a, own_at + r, value)

        @pl.when(c > 0)
        def _():
            value = part(r, c)
            for j in range(1, others):
                give(others - j, r).wait_recv()
                value = value + unpack(rs_in[j * crows + r].astype(F32), width)
            coarse_out[r, 0] = value
            put(ext_a, own_at + r, value)

        send_row(0, r)

    ids_r = lax.broadcasted_iota(jnp.int32, (width, width), 0)
    ids_c = lax.broadcasted_iota(jnp.int32, (width, width), 1)
    above = (ids_c > ids_r).astype(F32)
    below = (ids_c < ids_r).astype(F32)
    on = ids_c == ids_r

    for step in range(SWEEPS):
        ext = exts[step]
        old = coarse_out if step == 0 else factor_out
        steps = gather[step]
        for k in range(crows):
            pl.when(has_prev)(functools.partial(steps.first, 0, k))
            steps.second(1, k)
        for k in range(crows):
            pl.when(has_prev)(functools.partial(steps.second, 0, k))
        for k in range(crows):
            steps.third(1, k)
            pl.when(has_prev)(functools.partial(steps.third, 0, k))

        def relax(r, carry, ext=ext, old=old, step=step):
            row = row_base + r
            column = mine(o_coarse + r * slots + c)
            value = coarse_out[r, 0]
            for m in range(1, slots):
                s = r * slots + m
                left = unpack(ext[(slots + m) * crows + r], width)
                right = unpack(ext[table[o_spot + s]], width)
                value = value - table[o_flag + s].astype(F32) * jnp.dot(
                    left, right, preferred_element_type=F32
                )
            low = jnp.full((width, width), jnp.where(row > column, 1, 0)) == 1
            up = jnp.full((width, width), jnp.where(row < column, 1, 0)) == 1
            before = old[r, 0]
            own_diag = unpack(ext[slots * crows + r].astype(F32), width)
            their_diag = unpack(ext[table[o_diag + r]].astype(F32), width)
            left = jnp.where(low, before, own_diag * below)
            right = jnp.where(up, before, their_diag * above)
            value = value - jnp.dot(
                left.astype(BF), right.astype(BF), preferred_element_type=F32
            )
            pivots = jnp.maximum(
                jnp.sum(jnp.where(on, their_diag, 0.0), axis=0, keepdims=True), 1.0
            )
            scaled = low | (jnp.logical_not(up) & (ids_c < ids_r))
            value = jnp.where(scaled, value / pivots, value)
            factor_out[r, 0] = value
            if step < SWEEPS - 1:
                put(exts[step + 1], own_at + r, value)
                send_row(step + 1, r)
            return carry

        lax.fori_loop(0, crows, relax, 0)

    push_all(lambda copy: copy.wait_send())
    each_side(halo.done)

    @pl.when(c > 0)
    def _():
        for r in range(crows):
            for j in range(1, others):
                give(j, r).wait_send()

    for step in range(SWEEPS):
        for k in range(crows):
            gather[step].done(1, k)

            @pl.when(has_prev)
            def _():
                gather[step].done(0, k)

            @pl.when(has_next)
            def _():
                onward(step, k).wait_send()


def on_device(groups, peers, fine_tiles, fine_cols, agg_of, prolong, coarse_cols):
    rows, width = prolong.shape[0], prolong.shape[-1]
    crows, slots = coarse_cols.shape
    assert SWEEPS == 2 and slots == peers == 4 and fine_tiles.shape[1] == 1
    ints = jnp.concatenate([agg_of, coarse_cols.reshape(-1), fine_cols.reshape(-1)])
    room = -(-ints.shape[0] // 128) * 128
    ints = jnp.pad(ints, (0, room - ints.shape[0])).reshape(1, room)
    share = rows // peers
    dma = pltpu.SemaphoreType.DMA
    tile = (width, width)
    packed = (width + width // 2, 2 * width // 3)
    out = jax.ShapeDtypeStruct((crows, 1) + tile, F32)
    vmem = pl.BlockSpec(memory_space=pltpu.VMEM)
    anywhere = pl.BlockSpec(memory_space=pl.ANY)
    return pl.pallas_call(
        functools.partial(kernel, (groups, peers, rows, crows, slots, width)),
        out_shape=(out, out),
        in_specs=[vmem, anywhere, anywhere],
        out_specs=(vmem, vmem),
        scratch_shapes=[
            pltpu.VMEM((rows,) + tile, BF),
            pltpu.VMEM((rows,) + tile, BF),
            pltpu.VMEM((3 * rows,) + packed, BF),
            pltpu.VMEM((rows,) + tile, F32),
            pltpu.VMEM((slots * crows,) + packed, BF),
            pltpu.VMEM((slots * crows,) + packed, BF),
            pltpu.VMEM((2 * slots * crows,) + packed, BF),
            pltpu.VMEM((2 * slots * crows,) + packed, BF),
            pltpu.VMEM((3, 1, room), jnp.int32),
            pltpu.SMEM((3, 1, room), jnp.int32),
            pltpu.SMEM((rows,), jnp.int32),
            pltpu.SMEM((2 * rows,), jnp.int32),
            pltpu.SMEM((4 * crows * slots + crows,), jnp.int32),
            dma((peers + 1,)), dma((3,)), dma((2,)), dma((2,)),
            dma((2, 4, share)), dma((2, 4, share)),
            dma((slots, crows)), dma((slots, crows)),
            dma((2, 4, crows)), dma((2, 4, crows)),
            dma((2, 4, crows)), dma((2, 4, crows)),
        ],
        compiler_params=pltpu.CompilerParams(
            collective_id=0, has_side_effects=True, vmem_limit_bytes=56 * 1024 * 1024
        ),
    )(ints, fine_tiles.reshape((rows,) + tile), prolong)


def solution(mesh):
    in_specs = (
        P("agg", "col", None, None),
        P("agg", "col"),
        P("agg"),
        P("agg", None, None),
        P("agg", None),
    )
    out_specs = (P("agg", "col", None, None), P("agg", "col", None, None))
    return jax.shard_map(
        functools.partial(on_device, mesh.shape["agg"], mesh.shape["col"]),
        mesh=mesh, in_specs=in_specs, out_specs=out_specs, check_vma=False,
    )
```

```python
import functools

import jax
import jax.numpy as jnp
from jax import lax
from jax.experimental import pallas as pl
from jax.experimental.pallas import tpu as pltpu
from jax.sharding import PartitionSpec as P

SWEEPS = 2
MESH = pl.DeviceIdType.MESH
BF = jnp.bfloat16
F32 = jnp.float32


def pack(tile, dtype):
    width = tile.shape[-1]
    lanes = 2 * width // 3
    half = width // 2
    rest = tile[:, lanes:]
    return tile[:, :lanes].astype(dtype), jnp.concatenate([rest[:half], rest[half:]], axis=1).astype(dtype)


def put(ref, index, tile):
    left, rest = pack(tile, ref.dtype)
    width = tile.shape[-1]
    ref[index, 0:width] = left
    ref[index, width:] = rest


def unpack(tile, width):
    half = width // 2
    rest = tile[width:]
    fold = width - tile.shape[-1]
    right = jnp.concatenate([rest[:, :fold], rest[:, fold:]], axis=0)
    return jnp.concatenate([tile[:width], right], axis=1)


def kernel(
    dims, ints, fine_hbm, prolong_hbm, coarse_out, factor_out,
    fine, own_prolong, turned, near, seg, rs_out, rs_in, ext_a, ext_b, tab_v, tab, cls, order, table,
    in_sem, t_sem, t_send, t_recv,
    h_send, h_recv, r_send, r_recv, a_send, a_recv, b_send, b_recv,
):
    groups, peers, rows, crows, slots, width = dims
    a = lax.axis_index("agg")
    c = lax.axis_index("col")
    c1 = c + 1 - 2 * (c % 2)
    c2 = (c + 2) % peers
    c3 = c2 + 1 - 2 * (c2 % 2)
    has_prev = a > 0
    has_next = a < groups - 1
    parity = a % 2
    partner_agg = a + 1 - 2 * parity
    relay_to = a + 2 - 4 * parity
    relay_from = a - 2 + 4 * parity
    can_relay = (relay_to >= 0) & (relay_to < groups)
    has_other = (relay_from >= 0) & (relay_from < groups)
    alone = rows // (2 * peers)
    both = rows // 4
    direct = alone + both
    o_coarse = rows
    o_fine = o_coarse + crows * slots
    o_last = 0
    o_some = o_last + crows * slots
    o_spot = o_some + crows * slots
    o_flag = o_spot + crows * slots
    o_diag = o_flag + crows * slots

    blocks = [(c * alone, alone), (peers * alone + (c % 2) * both, both)]
    blocks += [(other * alone, alone) for other in (c1, c2, c3)]
    blocks += [(peers * alone + (c1 % 2) * both, both)]

    def take(j):
        start, size = blocks[j]
        return pltpu.make_async_copy(
            prolong_hbm.at[pl.ds(start, size)], own_prolong.at[pl.ds(start, size)], in_sem.at[j]
        )

    for j in range(len(blocks)):
        take(j).start()
    take_fine = pltpu.make_async_copy(fine_hbm, fine, in_sem.at[6])
    take_fine.start()

    barrier = pltpu.get_barrier_semaphore()
    for other in (c1, c2, c3):
        pl.semaphore_signal(barrier, inc=1, device_id=(a, other), device_id_type=MESH)

    @pl.when(has_prev)
    def _():
        pl.semaphore_signal(barrier, inc=1, device_id=(a - 1, c), device_id_type=MESH)

    @pl.when(has_next)
    def _():
        pl.semaphore_signal(barrier, inc=1, device_id=(a + 1, c), device_id_type=MESH)

    @pl.when(can_relay)
    def _():
        pl.semaphore_signal(barrier, inc=1, device_id=(relay_to, c), device_id_type=MESH)

    @pl.when(has_other)
    def _():
        pl.semaphore_signal(barrier, inc=1, device_id=(relay_from, c), device_id_type=MESH)

    def remote(src, dst, send, recv, device):
        return pltpu.make_async_remote_copy(
            src_ref=src, dst_ref=dst, send_sem=send, recv_sem=recv,
            device_id=device, device_id_type=MESH,
        )

    def pack_own(j):
        start, size = blocks[j]

        def body(k, carry):
            put(near, rows + start + k, own_prolong[start + k].astype(F32))
            return carry
        lax.fori_loop(0, size, body, 0)

    for j in range(2):
        take(j).wait()
        pack_own(j)

    @pl.when((a > 1) & (a < groups - 2))
    def _():
        pl.semaphore_wait(barrier, 7)

    @pl.when((a == 1) | (a == groups - 2))
    def _():
        pl.semaphore_wait(barrier, 6)

    @pl.when((a == 0) | (a == groups - 1))
    def _():
        pl.semaphore_wait(barrier, 5)

    def ints_to(g, device):
        return remote(ints, tab_v.at[2 - 2 * g], t_send.at[g], t_recv.at[1 - g], device)

    def tile_of(who, k):
        if k < alone:
            return who * alone + k
        return peers * alone + (who % 2) * both + k - alone

    def block_at(side):
        return ((1 - parity) if side == 0 else parity) * 2 * rows

    def push(k):
        src = near.at[pl.ds(rows + tile_of(c, k), 1)]
        dst = near.at[pl.ds(parity * 2 * rows + tile_of(c, k), 1)]
        return remote(src, dst, h_send.at[0, 0, k], h_recv.at[0, 0, k], (partner_agg, c))

    def relay(k):
        src = near.at[pl.ds(block_at(0) + tile_of(c, k), 1)]
        dst = near.at[pl.ds(parity * 2 * rows + tile_of(c, k), 1)]
        return remote(src, dst, h_send.at[1, 0, k], h_recv.at[1, 0, k], (relay_to, c))

    def pass_on(side, kind, who, k, device):
        view = near.at[pl.ds(block_at(side) + tile_of(who, k), 1)]
        return remote(view, view, h_send.at[side, kind, k], h_recv.at[side, kind, k], device)

    def arrived(side, k):
        pass_on(side, 0, c, k, (a, c1)).wait_recv()
        if side == 0:
            @pl.when(can_relay)
            def _():
                relay(k).start()
        if k < alone:
            pass_on(side, 2, c, k, (a, c2)).start()
        pass_on(side, 1, c, k, (a, c1)).start()

    def crossed(side, k):
        pass_on(side, 2, c2, k, (a, c2)).wait_recv()
        pass_on(side, 3, c2, k, (a, c1)).start()

    def complete(side):
        for k in range(direct):
            pass_on(side, 1, c1, k, (a, c1)).wait_recv()
            if k < alone:
                pass_on(side, 3, c3, k, (a, c1)).wait_recv()

    def left(side):
        for k in range(direct):
            pass_on(side, 1, c, k, (a, c1)).wait_send()
            if k < alone:
                pass_on(side, 2, c, k, (a, c2)).wait_send()
                pass_on(side, 3, c2, k, (a, c1)).wait_send()

    def other_side(step, *args):
        pl.when(has_other)(functools.partial(step, 1, *args))

    def ints_all(act):
        @pl.when(has_next)
        def _():
            act(ints_to(1, (a + 1, c)))

        @pl.when(has_prev)
        def _():
            act(ints_to(0, (a - 1, c)))

    for k in range(direct):
        push(k).start()
    ints_all(lambda copy: copy.start())
    for j in range(2, len(blocks)):
        take(j).wait()
        pack_own(j)

    relayed = crows // 2

    def spreader(buf, at, send, recv):
        def hop(g, kind, who, k, device):
            view = buf.at[pl.ds(at(g, who) + k, 1)]
            return remote(view, view, send.at[g, kind, k], recv.at[g, kind, k], device)

        class Steps:
            def share(g, k):
                if g == 1 or k >= relayed:
                    hop(g, 2, c, k, (a, c2)).start()
                hop(g, 1, c, k, (a, c1)).start()

            def first(g, k):
                hop(g, 0, c, k, (a, c1)).wait_recv()
                Steps.share(g, k)

            def beyond(k):
                src = buf.at[pl.ds(at(1, c2) + k, 1)]
                dst = buf.at[pl.ds(at(0, c2) + k, 1)]
                return remote(src, dst, send.at[0, 4, k], recv.at[0, 4, k], (a + 1, c))

            def second(g, k):
                direct_row = g == 0 and k < relayed
                hop(g, 4 if direct_row else 2, c2, k, (a, c2)).wait_recv()
                if g == 1 and k < relayed:
                    @pl.when(has_next)
                    def _():
                        Steps.beyond(k).start()
                hop(g, 3, c2, k, (a, c1)).start()

            def third(g, k):
                hop(g, 1, c1, k, (a, c1)).wait_recv()
                hop(g, 3, c3, k, (a, c1)).wait_recv()

            def done(g, k):
                if g == 1 or k >= relayed:
                    hop(g, 2, c, k, (a, c2)).wait_send()
                hop(g, 1, c, k, (a, c1)).wait_send()
                hop(g, 3, c2, k, (a, c1)).wait_send()

        return Steps

    def to_scalar(g):
        return pltpu.make_async_copy(tab_v.at[g], tab.at[g], t_sem.at[g])

    own_ints = pltpu.make_async_copy(ints, tab.at[1], t_sem.at[1])
    own_ints.start()

    lag = 2
    for k in range(direct + lag):
        if k < direct:
            arrived(0, k)
        if k >= lag:
            other_side(arrived, k - lag)

    def turn(i, carry):
        turned[i] = own_prolong[i].astype(F32).T.astype(BF)
        return carry

    lax.fori_loop(0, rows, turn, 0)
    own_ints.wait()

    @pl.when(has_prev)
    def _():
        ints_to(1, (a - 1, c)).wait_recv()
        to_scalar(0).start()
        to_scalar(0).wait()

    @pl.when(has_next)
    def _():
        ints_to(0, (a + 1, c)).wait_recv()
        to_scalar(2).start()
        to_scalar(2).wait()

    row_base = a * crows
    ext_base = row_base - crows

    def mine(k):
        return tab[1, 0, k]

    def place_of(i):
        return mine(o_fine + i) - (a - 1) * rows

    def classify(i, carry):
        place = jnp.clip(place_of(i), 0, 3 * rows - 1)
        target = tab[place // rows, 0, place % rows]
        r = jnp.clip(mine(i) - row_base, 0, crows - 1)
        q = 0
        for s in range(1, slots):
            q = jnp.where(mine(o_coarse + r * slots + s) == target, s, q)
        cls[i] = (r * slots + q) * rows + i
        return carry

    lax.fori_loop(0, rows, classify, 0)

    def rank(i, carry):
        key = cls[i]
        below = 0
        for j in range(rows):
            below = below + jnp.where(cls[j] < key, 1, 0)
        order[rows + i] = below
        return carry

    lax.fori_loop(0, rows, rank, 0)

    def place_key(k, carry):
        key = 0
        for i in range(rows):
            key = key + jnp.where(order[rows + i] == k, cls[i], 0)
        order[k] = key
        return carry

    lax.fori_loop(0, rows, place_key, 0)

    def ends(s, carry):
        upto = 0
        some = 0
        for i in range(rows):
            own_class = cls[i] // rows
            upto = upto + jnp.where(own_class <= s, 1, 0)
            some = jnp.where(own_class == s, 1, some)
        table[o_last + s] = jnp.maximum(upto - 1, 0)
        table[o_some + s] = some
        return carry

    lax.fori_loop(0, crows * slots, ends, 0)

    def ties(r, carry):
        row = row_base + r
        column = mine(o_coarse + r * slots + c)
        lowest = jnp.minimum(row, column)
        for m in range(1, slots):
            prior = mine(o_coarse + r * slots + m)
            k = jnp.clip(prior - ext_base, 0, 2 * crows - 1)
            g = k // crows
            slot = 0
            found = 0
            for n in range(slots):
                same = tab[g, 0, o_coarse + (k % crows) * slots + n] == column
                slot = jnp.where(same, n, slot)
                found = jnp.where(same, 1, found)
            found = jnp.where(prior < lowest, found, 0)
            spot = (g * slots + slot) * crows + k % crows
            table[o_spot + r * slots + m] = jnp.where(found == 1, spot, slots * crows)
            table[o_flag + r * slots + m] = found
        k = jnp.clip(column - ext_base, 0, 2 * crows - 1)
        table[o_diag + r] = jnp.where(
            column < row, (k // crows) * slots * crows + k % crows, slots * crows + r
        )
        return carry

    lax.fori_loop(0, crows, ties, 0)

    for k in range(alone):
        crossed(0, k)
    for k in range(alone):
        other_side(crossed, k)
    take_fine.wait()
    complete(0)
    other_side(complete)

    def lift(k, total):
        key = order[k]
        i = key % rows
        earlier = order[jnp.maximum(k - 1, 0)]
        goes_on = jnp.where(earlier // rows == key // rows, 1, 0)
        place = jnp.clip(place_of(i), 0, 3 * rows - 1)
        carried = jnp.dot(
            fine[i], unpack(near[place], width), preferred_element_type=F32
        ).astype(BF)
        lifted = jnp.dot(turned[i], carried, preferred_element_type=F32)
        total = lifted + total * goes_on.astype(F32)
        seg[k] = total
        return total

    lax.fori_loop(0, rows, lift, jnp.zeros((width, width), F32), unroll=4)

    def part(r, q):
        s = r * slots + q
        return seg[table[o_last + s]] * table[o_some + s].astype(F32)

    others = slots - 1

    def partner(j):
        return 1 + (c - 1 + j) % others

    def give(j, r):
        return remote(
            rs_out.at[pl.ds(j * crows + r, 1)], rs_in.at[pl.ds((others - j) * crows + r, 1)],
            r_send.at[j, r], r_recv.at[others - j, r], (a, partner(j)),
        )

    @pl.when(c > 0)
    def _():
        for r in range(crows):
            for j in range(1, others):
                put(rs_out, j * crows + r, part(r, partner(j)))
                give(j, r).start()

    own_at = (slots + c) * crows
    exts = (ext_a, ext_b)
    gather = [
        spreader(ext, lambda g, who: (g * slots + who) * crows, send, recv)
        for ext, send, recv in ((ext_a, a_send, a_recv), (ext_b, b_send, b_recv))
    ]

    def onward(step, r):
        send, recv = ((a_send, a_recv), (b_send, b_recv))[step]
        ext = exts[step]
        return remote(
            ext.at[pl.ds(own_at + r, 1)], ext.at[pl.ds(c * crows + r, 1)],
            send.at[0, 0, r], recv.at[0, 0, r], (a + 1, c),
        )

    def send_row(step, r):
        gather[step].share(1, r)

        @pl.when(has_next)
        def _():
            onward(step, r).start()

    for r in range(crows):
        @pl.when(c == 0)
        def _():
            value = part(r, 0)
            coarse_out[r, 0] = value
            put(ext_a, own_at + r, value)

        @pl.when(c > 0)
        def _():
            value = part(r, c)
            for j in range(1, others):
                give(others - j, r).wait_recv()
                value = value + unpack(rs_in[j * crows + r].astype(F32), width)
            coarse_out[r, 0] = value
            put(ext_a, own_at + r, value)

        send_row(0, r)

    ids_r = lax.broadcasted_iota(jnp.int32, (width, width), 0)
    ids_c = lax.broadcasted_iota(jnp.int32, (width, width), 1)
    above = (ids_c > ids_r).astype(F32)
    below = (ids_c < ids_r).astype(F32)
    on = ids_c == ids_r

    for step in range(SWEEPS):
        ext = exts[step]
        old = coarse_out if step == 0 else factor_out
        steps = gather[step]
        for k in range(crows):
            steps.second(1, k)
            pl.when(has_prev)(functools.partial(steps.first, 0, k))
        for k in range(crows):
            pl.when(has_prev)(functools.partial(steps.second, 0, k))
        for k in range(crows):
            steps.third(1, k)
            pl.when(has_prev)(functools.partial(steps.third, 0, k))

        def relax(r, carry, ext=ext, old=old, step=step):
            row = row_base + r
            column = mine(o_coarse + r * slots + c)
            value = coarse_out[r, 0]
            for m in range(1, slots):
                s = r * slots + m
                left = unpack(ext[(slots + m) * crows + r], width)
                right = unpack(ext[table[o_spot + s]], width)
                value = value - table[o_flag + s].astype(F32) * jnp.dot(
                    left, right, preferred_element_type=F32
                )
            low = jnp.full((width, width), jnp.where(row > column, 1, 0)) == 1
            up = jnp.full((width, width), jnp.where(row < column, 1, 0)) == 1
            before = old[r, 0]
            own_diag = unpack(ext[slots * crows + r].astype(F32), width)
            their_diag = unpack(ext[table[o_diag + r]].astype(F32), width)
            left = jnp.where(low, before, own_diag * below)
            right = jnp.where(up, before, their_diag * above)
            value = value - jnp.dot(
                left.astype(BF), right.astype(BF), preferred_element_type=F32
            )
            pivots = jnp.maximum(
                jnp.sum(jnp.where(on, their_diag, 0.0), axis=0, keepdims=True), 1.0
            )
            scaled = low | (jnp.logical_not(up) & (ids_c < ids_r))
            value = jnp.where(scaled, value / pivots, value)
            factor_out[r, 0] = value
            if step < SWEEPS - 1:
                put(exts[step + 1], own_at + r, value)
                send_row(step + 1, r)
            return carry

        lax.fori_loop(0, crows, relax, 0)

    ints_all(lambda copy: copy.wait_send())
    for k in range(direct):
        push(k).wait_send()

    @pl.when(can_relay)
    def _():
        for k in range(direct):
            relay(k).wait_send()

    left(0)
    other_side(left)

    @pl.when(c > 0)
    def _():
        for r in range(crows):
            for j in range(1, others):
                give(j, r).wait_send()

    for step in range(SWEEPS):
        for k in range(crows):
            gather[step].done(1, k)

            @pl.when(has_prev)
            def _():
                gather[step].done(0, k)

            @pl.when(has_next)
            def _():
                onward(step, k).wait_send()
                if k < relayed:
                    gather[step].beyond(k).wait_send()


def on_device(groups, peers, fine_tiles, fine_cols, agg_of, prolong, coarse_cols):
    rows, width = prolong.shape[0], prolong.shape[-1]
    crows, slots = coarse_cols.shape
    assert SWEEPS == 2 and slots == peers == 4 and fine_tiles.shape[1] == 1
    ints = jnp.concatenate([agg_of, coarse_cols.reshape(-1), fine_cols.reshape(-1)])
    room = -(-ints.shape[0] // 128) * 128
    ints = jnp.pad(ints, (0, room - ints.shape[0])).reshape(1, room)
    assert groups % 2 == 0 and groups >= 4
    direct = rows // (2 * peers) + rows // 4
    dma = pltpu.SemaphoreType.DMA
    tile = (width, width)
    packed = (width + width // 2, 2 * width // 3)
    out = jax.ShapeDtypeStruct((crows, 1) + tile, F32)
    vmem = pl.BlockSpec(memory_space=pltpu.VMEM)
    anywhere = pl.BlockSpec(memory_space=pl.ANY)
    return pl.pallas_call(
        functools.partial(kernel, (groups, peers, rows, crows, slots, width)),
        out_shape=(out, out),
        in_specs=[vmem, anywhere, anywhere],
        out_specs=(vmem, vmem),
        scratch_shapes=[
            pltpu.VMEM((rows,) + tile, BF),
            pltpu.VMEM((rows,) + tile, BF),
            pltpu.VMEM((rows,) + tile, BF),
            pltpu.VMEM((3 * rows,) + packed, BF),
            pltpu.VMEM((rows,) + tile, F32),
            pltpu.VMEM((slots * crows,) + packed, BF),
            pltpu.VMEM((slots * crows,) + packed, BF),
            pltpu.VMEM((2 * slots * crows,) + packed, BF),
            pltpu.VMEM((2 * slots * crows,) + packed, BF),
            pltpu.VMEM((3, 1, room), jnp.int32),
            pltpu.SMEM((3, 1, room), jnp.int32),
            pltpu.SMEM((rows,), jnp.int32),
            pltpu.SMEM((2 * rows,), jnp.int32),
            pltpu.SMEM((4 * crows * slots + crows,), jnp.int32),
            dma((7,)), dma((3,)), dma((2,)), dma((2,)),
            dma((2, 4, direct)), dma((2, 4, direct)),
            dma((slots, crows)), dma((slots, crows)),
            dma((2, 5, crows)), dma((2, 5, crows)),
            dma((2, 5, crows)), dma((2, 5, crows)),
        ],
        compiler_params=pltpu.CompilerParams(
            collective_id=0, has_side_effects=True, vmem_limit_bytes=56 * 1024 * 1024
        ),
    )(ints, fine_tiles.reshape((rows,) + tile), prolong)


def solution(mesh):
    in_specs = (
        P("agg", "col", None, None),
        P("agg", "col"),
        P("agg"),
        P("agg", None, None),
        P("agg", None),
    )
    out_specs = (P("agg", "col", None, None), P("agg", "col", None, None))
    return jax.shard_map(
        functools.partial(on_device, mesh.shape["agg"], mesh.shape["col"]),
        mesh=mesh, in_specs=in_specs, out_specs=out_specs, check_vma=False,
    )
```

```python
import functools

import jax
import jax.numpy as jnp
from jax import lax
from jax.experimental import pallas as pl
from jax.experimental.pallas import tpu as pltpu
from jax.sharding import PartitionSpec as P

SWEEPS = 2
MESH = pl.DeviceIdType.MESH
BF = jnp.bfloat16
F32 = jnp.float32


def pack(tile, dtype):
    width = tile.shape[-1]
    lanes = 2 * width // 3
    half = width // 2
    rest = tile[:, lanes:]
    return tile[:, :lanes].astype(dtype), jnp.concatenate([rest[:half], rest[half:]], axis=1).astype(dtype)


def put(ref, index, tile):
    left, rest = pack(tile, ref.dtype)
    width = tile.shape[-1]
    ref[index, 0:width] = left
    ref[index, width:] = rest


def unpack(tile, width):
    half = width // 2
    rest = tile[width:]
    fold = width - tile.shape[-1]
    right = jnp.concatenate([rest[:, :fold], rest[:, fold:]], axis=0)
    return jnp.concatenate([tile[:width], right], axis=1)


def kernel(
    dims, ints, fine_hbm, prolong_hbm, coarse_out, factor_out,
    fine, own_prolong, turned, near, seg, rs_out, rs_in, ext_a, ext_b, tab_v, tab, cls, order, table,
    in_sem, t_sem, t_send, t_recv,
    h_send, h_recv, r_send, r_recv, a_send, a_recv, b_send, b_recv,
):
    groups, peers, rows, crows, slots, width = dims
    a = lax.axis_index("agg")
    c = lax.axis_index("col")
    c1 = c + 1 - 2 * (c % 2)
    c2 = (c + 2) % peers
    c3 = c2 + 1 - 2 * (c2 % 2)
    has_prev = a > 0
    has_next = a < groups - 1
    parity = a % 2
    partner_agg = a + 1 - 2 * parity
    relay_to = a + 2 - 4 * parity
    relay_from = a - 2 + 4 * parity
    can_relay = (relay_to >= 0) & (relay_to < groups)
    has_other = (relay_from >= 0) & (relay_from < groups)
    alone = rows // (2 * peers)
    both = rows // 4
    direct = alone + both
    o_coarse = rows
    o_fine = o_coarse + crows * slots
    o_last = 0
    o_some = o_last + crows * slots
    o_spot = o_some + crows * slots
    o_flag = o_spot + crows * slots
    o_diag = o_flag + crows * slots

    blocks = [(c * alone, alone), (peers * alone + (c % 2) * both, both)]
    blocks += [(other * alone, alone) for other in (c1, c2, c3)]
    blocks += [(peers * alone + (c1 % 2) * both, both)]

    def take(j):
        start, size = blocks[j]
        return pltpu.make_async_copy(
            prolong_hbm.at[pl.ds(start, size)], own_prolong.at[pl.ds(start, size)], in_sem.at[j]
        )

    for j in range(len(blocks)):
        take(j).start()
    take_fine = pltpu.make_async_copy(fine_hbm, fine, in_sem.at[6])
    take_fine.start()

    barrier = pltpu.get_barrier_semaphore()
    for other in (c1, c2, c3):
        pl.semaphore_signal(barrier, inc=1, device_id=(a, other), device_id_type=MESH)

    @pl.when(has_prev)
    def _():
        pl.semaphore_signal(barrier, inc=1, device_id=(a - 1, c), device_id_type=MESH)

    @pl.when(has_next)
    def _():
        pl.semaphore_signal(barrier, inc=1, device_id=(a + 1, c), device_id_type=MESH)

    @pl.when(can_relay)
    def _():
        pl.semaphore_signal(barrier, inc=1, device_id=(relay_to, c), device_id_type=MESH)

    @pl.when(has_other)
    def _():
        pl.semaphore_signal(barrier, inc=1, device_id=(relay_from, c), device_id_type=MESH)

    def remote(src, dst, send, recv, device):
        return pltpu.make_async_remote_copy(
            src_ref=src, dst_ref=dst, send_sem=send, recv_sem=recv,
            device_id=device, device_id_type=MESH,
        )

    def pack_own(j):
        start, size = blocks[j]

        def body(k, carry):
            put(near, rows + start + k, own_prolong[start + k].astype(F32))
            return carry
        lax.fori_loop(0, size, body, 0)

    for j in range(2):
        take(j).wait()
        pack_own(j)

    @pl.when((a > 1) & (a < groups - 2))
    def _():
        pl.semaphore_wait(barrier, 7)

    @pl.when((a == 1) | (a == groups - 2))
    def _():
        pl.semaphore_wait(barrier, 6)

    @pl.when((a == 0) | (a == groups - 1))
    def _():
        pl.semaphore_wait(barrier, 5)

    def ints_to(g, device):
        return remote(ints, tab_v.at[2 - 2 * g], t_send.at[g], t_recv.at[1 - g], device)

    def tile_of(who, k):
        if k < alone:
            return who * alone + k
        return peers * alone + (who % 2) * both + k - alone

    def block_at(side):
        return ((1 - parity) if side == 0 else parity) * 2 * rows

    def push(k):
        src = near.at[pl.ds(rows + tile_of(c, k), 1)]
        dst = near.at[pl.ds(parity * 2 * rows + tile_of(c, k), 1)]
        return remote(src, dst, h_send.at[0, 0, k], h_recv.at[0, 0, k], (partner_agg, c))

    def relay(k):
        src = near.at[pl.ds(block_at(0) + tile_of(c, k), 1)]
        dst = near.at[pl.ds(parity * 2 * rows + tile_of(c, k), 1)]
        return remote(src, dst, h_send.at[1, 0, k], h_recv.at[1, 0, k], (relay_to, c))

    def pass_on(side, kind, who, k, device):
        view = near.at[pl.ds(block_at(side) + tile_of(who, k), 1)]
        return remote(view, view, h_send.at[side, kind, k], h_recv.at[side, kind, k], device)

    def arrived(side, k):
        pass_on(side, 0, c, k, (a, c1)).wait_recv()
        if side == 0:
            @pl.when(can_relay)
            def _():
                relay(k).start()
        if k < alone:
            pass_on(side, 2, c, k, (a, c2)).start()
        pass_on(side, 1, c, k, (a, c1)).start()

    def crossed(side, k):
        pass_on(side, 2, c2, k, (a, c2)).wait_recv()
        pass_on(side, 3, c2, k, (a, c1)).start()

    def complete(side):
        for k in range(direct):
            pass_on(side, 1, c1, k, (a, c1)).wait_recv()
            if k < alone:
                pass_on(side, 3, c3, k, (a, c1)).wait_recv()

    def left(side):
        for k in range(direct):
            pass_on(side, 1, c, k, (a, c1)).wait_send()
            if k < alone:
                pass_on(side, 2, c, k, (a, c2)).wait_send()
                pass_on(side, 3, c2, k, (a, c1)).wait_send()

    def other_side(step, *args):
        pl.when(has_other)(functools.partial(step, 1, *args))

    def ints_all(act):
        @pl.when(has_next)
        def _():
            act(ints_to(1, (a + 1, c)))

        @pl.when(has_prev)
        def _():
            act(ints_to(0, (a - 1, c)))

    ints_all(lambda copy: copy.start())
    for k in range(direct):
        push(k).start()
    for j in range(2, len(blocks)):
        take(j).wait()
        pack_own(j)

    relayed = crows // 2

    def spreader(buf, at, send, recv):
        def hop(g, kind, who, k, device):
            view = buf.at[pl.ds(at(g, who) + k, 1)]
            return remote(view, view, send.at[g, kind, k], recv.at[g, kind, k], device)

        class Steps:
            def share(g, k):
                if g == 1 or k >= relayed:
                    hop(g, 2, c, k, (a, c2)).start()
                hop(g, 1, c, k, (a, c1)).start()

            def first(g, k):
                hop(g, 0, c, k, (a, c1)).wait_recv()
                Steps.share(g, k)

            def beyond(k):
                src = buf.at[pl.ds(at(1, c2) + k, 1)]
                dst = buf.at[pl.ds(at(0, c2) + k, 1)]
                return remote(src, dst, send.at[0, 4, k], recv.at[0, 4, k], (a + 1, c))

            def second(g, k):
                direct_row = g == 0 and k < relayed
                hop(g, 4 if direct_row else 2, c2, k, (a, c2)).wait_recv()
                if g == 1 and k < relayed:
                    @pl.when(has_next)
                    def _():
                        Steps.beyond(k).start()
                hop(g, 3, c2, k, (a, c1)).start()

            def third(g, k):
                hop(g, 1, c1, k, (a, c1)).wait_recv()
                hop(g, 3, c3, k, (a, c1)).wait_recv()

            def done(g, k):
                if g == 1 or k >= relayed:
                    hop(g, 2, c, k, (a, c2)).wait_send()
                hop(g, 1, c, k, (a, c1)).wait_send()
                hop(g, 3, c2, k, (a, c1)).wait_send()

        return Steps

    def to_scalar(g):
        return pltpu.make_async_copy(tab_v.at[g], tab.at[g], t_sem.at[g])

    own_ints = pltpu.make_async_copy(ints, tab.at[1], t_sem.at[1])
    own_ints.start()

    lag = 2
    for k in range(direct + lag):
        if k < direct:
            arrived(0, k)
        if k >= lag:
            other_side(arrived, k - lag)
        for i in range(k * rows // (direct + lag), (k + 1) * rows // (direct + lag)):
            turned[i] = own_prolong[i].astype(F32).T.astype(BF)
        if 0 <= k - 3 < alone:
            crossed(0, k - 3)
        if 0 <= k - 5 < alone:
            other_side(crossed, k - 5)
    own_ints.wait()

    @pl.when(has_prev)
    def _():
        ints_to(1, (a - 1, c)).wait_recv()
        to_scalar(0).start()
        to_scalar(0).wait()

    @pl.when(has_next)
    def _():
        ints_to(0, (a + 1, c)).wait_recv()
        to_scalar(2).start()
        to_scalar(2).wait()

    row_base = a * crows
    ext_base = row_base - crows

    def mine(k):
        return tab[1, 0, k]

    def place_of(i):
        return mine(o_fine + i) - (a - 1) * rows

    def classify(i, carry):
        place = jnp.clip(place_of(i), 0, 3 * rows - 1)
        target = tab[place // rows, 0, place % rows]
        r = jnp.clip(mine(i) - row_base, 0, crows - 1)
        q = 0
        for s in range(1, slots):
            q = jnp.where(mine(o_coarse + r * slots + s) == target, s, q)
        cls[i] = (r * slots + q) * rows + i
        return carry

    lax.fori_loop(0, rows, classify, 0)

    def rank(i, carry):
        key = cls[i]
        below = 0
        for j in range(rows):
            below = below + jnp.where(cls[j] < key, 1, 0)
        order[rows + i] = below
        return carry

    lax.fori_loop(0, rows, rank, 0)

    def place_key(k, carry):
        key = 0
        for i in range(rows):
            key = key + jnp.where(order[rows + i] == k, cls[i], 0)
        order[k] = key
        return carry

    lax.fori_loop(0, rows, place_key, 0)

    def ends(s, carry):
        upto = 0
        some = 0
        for i in range(rows):
            own_class = cls[i] // rows
            upto = upto + jnp.where(own_class <= s, 1, 0)
            some = jnp.where(own_class == s, 1, some)
        table[o_last + s] = jnp.maximum(upto - 1, 0)
        table[o_some + s] = some
        return carry

    lax.fori_loop(0, crows * slots, ends, 0)

    def ties(r, carry):
        row = row_base + r
        column = mine(o_coarse + r * slots + c)
        lowest = jnp.minimum(row, column)
        for m in range(1, slots):
            prior = mine(o_coarse + r * slots + m)
            k = jnp.clip(prior - ext_base, 0, 2 * crows - 1)
            g = k // crows
            slot = 0
            found = 0
            for n in range(slots):
                same = tab[g, 0, o_coarse + (k % crows) * slots + n] == column
                slot = jnp.where(same, n, slot)
                found = jnp.where(same, 1, found)
            found = jnp.where(prior < lowest, found, 0)
            spot = (g * slots + slot) * crows + k % crows
            table[o_spot + r * slots + m] = jnp.where(found == 1, spot, slots * crows)
            table[o_flag + r * slots + m] = found
        k = jnp.clip(column - ext_base, 0, 2 * crows - 1)
        table[o_diag + r] = jnp.where(
            column < row, (k // crows) * slots * crows + k % crows, slots * crows + r
        )
        return carry

    lax.fori_loop(0, crows, ties, 0)

    for k in range(max(direct + lag - 3, 0), alone):
        crossed(0, k)
    for k in range(max(direct + lag - 5, 0), alone):
        other_side(crossed, k)
    take_fine.wait()
    complete(0)
    other_side(complete)

    def lift(k, total):
        key = order[k]
        i = key % rows
        earlier = order[jnp.maximum(k - 1, 0)]
        goes_on = jnp.where(earlier // rows == key // rows, 1, 0)
        place = jnp.clip(place_of(i), 0, 3 * rows - 1)
        carried = jnp.dot(
            fine[i], unpack(near[place], width), preferred_element_type=F32
        ).astype(BF)
        lifted = jnp.dot(turned[i], carried, preferred_element_type=F32)
        total = lifted + total * goes_on.astype(F32)
        seg[k] = total
        return total

    lax.fori_loop(0, rows, lift, jnp.zeros((width, width), F32), unroll=4)

    def part(r, q):
        s = r * slots + q
        return seg[table[o_last + s]] * table[o_some + s].astype(F32)

    others = slots - 1

    def partner(j):
        return 1 + (c - 1 + j) % others

    def give(j, r):
        return remote(
            rs_out.at[pl.ds(j * crows + r, 1)], rs_in.at[pl.ds((others - j) * crows + r, 1)],
            r_send.at[j, r], r_recv.at[others - j, r], (a, partner(j)),
        )

    @pl.when(c > 0)
    def _():
        for r in range(crows):
            for j in range(1, others):
                put(rs_out, j * crows + r, part(r, partner(j)))
                give(j, r).start()

    own_at = (slots + c) * crows
    exts = (ext_a, ext_b)
    gather = [
        spreader(ext, lambda g, who: (g * slots + who) * crows, send, recv)
        for ext, send, recv in ((ext_a, a_send, a_recv), (ext_b, b_send, b_recv))
    ]

    def onward(step, r):
        send, recv = ((a_send, a_recv), (b_send, b_recv))[step]
        ext = exts[step]
        return remote(
            ext.at[pl.ds(own_at + r, 1)], ext.at[pl.ds(c * crows + r, 1)],
            send.at[0, 0, r], recv.at[0, 0, r], (a + 1, c),
        )

    def send_row(step, r):
        gather[step].share(1, r)

        @pl.when(has_next)
        def _():
            onward(step, r).start()

    for r in range(crows):
        @pl.when(c == 0)
        def _():
            value = part(r, 0)
            coarse_out[r, 0] = value
            put(ext_a, own_at + r, value)

        @pl.when(c > 0)
        def _():
            value = part(r, c)
            for j in range(1, others):
                give(others - j, r).wait_recv()
                value = value + unpack(rs_in[j * crows + r].astype(F32), width)
            coarse_out[r, 0] = value
            put(ext_a, own_at + r, value)

        send_row(0, r)

    ids_r = lax.broadcasted_iota(jnp.int32, (width, width), 0)
    ids_c = lax.broadcasted_iota(jnp.int32, (width, width), 1)
    above = (ids_c > ids_r).astype(F32)
    below = (ids_c < ids_r).astype(F32)
    on = ids_c == ids_r

    for step in range(SWEEPS):
        ext = exts[step]
        old = coarse_out if step == 0 else factor_out
        steps = gather[step]
        for k in range(crows):
            steps.second(1, k)
            pl.when(has_prev)(functools.partial(steps.first, 0, k))
        for k in range(crows):
            pl.when(has_prev)(functools.partial(steps.second, 0, k))
        for k in range(crows):
            steps.third(1, k)
            pl.when(has_prev)(functools.partial(steps.third, 0, k))

        def relax(r, carry, ext=ext, old=old, step=step):
            row = row_base + r
            column = mine(o_coarse + r * slots + c)
            value = coarse_out[r, 0]
            for m in range(1, slots):
                s = r * slots + m
                left = unpack(ext[(slots + m) * crows + r], width)
                right = unpack(ext[table[o_spot + s]], width)
                value = value - table[o_flag + s].astype(F32) * jnp.dot(
                    left, right, preferred_element_type=F32
                )
            low = jnp.full((width, width), jnp.where(row > column, 1, 0)) == 1
            up = jnp.full((width, width), jnp.where(row < column, 1, 0)) == 1
            before = old[r, 0]
            own_diag = unpack(ext[slots * crows + r].astype(F32), width)
            their_diag = unpack(ext[table[o_diag + r]].astype(F32), width)
            left = jnp.where(low, before, own_diag * below)
            right = jnp.where(up, before, their_diag * above)
            value = value - jnp.dot(
                left.astype(BF), right.astype(BF), preferred_element_type=F32
            )
            pivots = jnp.maximum(
                jnp.sum(jnp.where(on, their_diag, 0.0), axis=0, keepdims=True), 1.0
            )
            scaled = low | (jnp.logical_not(up) & (ids_c < ids_r))
            value = jnp.where(scaled, value / pivots, value)
            factor_out[r, 0] = value
            if step < SWEEPS - 1:
                put(exts[step + 1], own_at + r, value)
                send_row(step + 1, r)
            return carry

        lax.fori_loop(0, crows, relax, 0)

    ints_all(lambda copy: copy.wait_send())
    for k in range(direct):
        push(k).wait_send()

    @pl.when(can_relay)
    def _():
        for k in range(direct):
            relay(k).wait_send()

    left(0)
    other_side(left)

    @pl.when(c > 0)
    def _():
        for r in range(crows):
            for j in range(1, others):
                give(j, r).wait_send()

    for step in range(SWEEPS):
        for k in range(crows):
            gather[step].done(1, k)

            @pl.when(has_prev)
            def _():
                gather[step].done(0, k)

            @pl.when(has_next)
            def _():
                onward(step, k).wait_send()
                if k < relayed:
                    gather[step].beyond(k).wait_send()


def on_device(groups, peers, fine_tiles, fine_cols, agg_of, prolong, coarse_cols):
    rows, width = prolong.shape[0], prolong.shape[-1]
    crows, slots = coarse_cols.shape
    assert SWEEPS == 2 and slots == peers == 4 and fine_tiles.shape[1] == 1
    ints = jnp.concatenate([agg_of, coarse_cols.reshape(-1), fine_cols.reshape(-1)])
    room = -(-ints.shape[0] // 128) * 128
    ints = jnp.pad(ints, (0, room - ints.shape[0])).reshape(1, room)
    assert groups % 2 == 0 and groups >= 4
    direct = rows // (2 * peers) + rows // 4
    dma = pltpu.SemaphoreType.DMA
    tile = (width, width)
    packed = (width + width // 2, 2 * width // 3)
    out = jax.ShapeDtypeStruct((crows, 1) + tile, F32)
    vmem = pl.BlockSpec(memory_space=pltpu.VMEM)
    anywhere = pl.BlockSpec(memory_space=pl.ANY)
    return pl.pallas_call(
        functools.partial(kernel, (groups, peers, rows, crows, slots, width)),
        out_shape=(out, out),
        in_specs=[vmem, anywhere, anywhere],
        out_specs=(vmem, vmem),
        scratch_shapes=[
            pltpu.VMEM((rows,) + tile, BF),
            pltpu.VMEM((rows,) + tile, BF),
            pltpu.VMEM((rows,) + tile, BF),
            pltpu.VMEM((3 * rows,) + packed, BF),
            pltpu.VMEM((rows,) + tile, F32),
            pltpu.VMEM((slots * crows,) + packed, BF),
            pltpu.VMEM((slots * crows,) + packed, BF),
            pltpu.VMEM((2 * slots * crows,) + packed, BF),
            pltpu.VMEM((2 * slots * crows,) + packed, BF),
            pltpu.VMEM((3, 1, room), jnp.int32),
            pltpu.SMEM((3, 1, room), jnp.int32),
            pltpu.SMEM((rows,), jnp.int32),
            pltpu.SMEM((2 * rows,), jnp.int32),
            pltpu.SMEM((4 * crows * slots + crows,), jnp.int32),
            dma((7,)), dma((3,)), dma((2,)), dma((2,)),
            dma((2, 4, direct)), dma((2, 4, direct)),
            dma((slots, crows)), dma((slots, crows)),
            dma((2, 5, crows)), dma((2, 5, crows)),
            dma((2, 5, crows)), dma((2, 5, crows)),
        ],
        compiler_params=pltpu.CompilerParams(
            collective_id=0, has_side_effects=True, vmem_limit_bytes=56 * 1024 * 1024
        ),
    )(ints, fine_tiles.reshape((rows,) + tile), prolong)


def solution(mesh):
    in_specs = (
        P("agg", "col", None, None),
        P("agg", "col"),
        P("agg"),
        P("agg", None, None),
        P("agg", None),
    )
    out_specs = (P("agg", "col", None, None), P("agg", "col", None, None))
    return jax.shard_map(
        functools.partial(on_device, mesh.shape["agg"], mesh.shape["col"]),
        mesh=mesh, in_specs=in_specs, out_specs=out_specs, check_vma=False,
    )
```
